32 devices in a mesh: dev: 32 (over z, y, x, core).
Axes of the slice: x: 2, y: 2, z: 4, core: 2. Of those that a mesh axis runs over, the one named last changes fastest.
Arguments:
- field_in: float32 [32, 8, 128, 128], P(None, None, 'dev'), may hold values from -6 to 6
- source: float32 [32, 8, 128, 128], P(None, None, 'dev'), may hold values from -12 to 12
- cell_factor: float32 [8, 128, 128], P(None, 'dev'), may hold values from 0.5 to 2
- layer_material: int32 [8], replicated, may hold values from 0 to 3
- material_scale: float32 [4], replicated, may hold values from 0.25 to 4
- panel_cell: int32 [32768], P('dev'), may hold values from 0 to 16383
- panel_pos: float32 [3, 32768], replicated, may hold values from 0 to 1
- panel_area: float32 [32768], replicated, may hold values from 0.5 to 2
- flux_in: float32 [32, 32768], P(None, 'dev'), may hold values from -6 to 6
- pair_list: int32 [128, 2], P('dev'), may hold values from -1 to 15, as said below
Outputs:
- field_out: float32 [32, 8, 128, 128], P(None, None, 'dev')
- flux_out: float32 [32, 32768], P(None, 'dev')
The draws below stay inside these ranges and needn't reach their ends.
Inputs may be any that keep to these rules, and one draw needn't show every extreme that they name: `pair_list`: each row is a tile pair (i, j) with i >= j, or (-1, -1) for an empty slot. No pair is listed twice. In each device's 4 rows the pairs come first, then the empty slots; at least a quarter of every device's slots are filled, and some device has all 4 filled.
All inputs are finite; a program needn't handle non-finite values.
Results may differ from the reference program's by a relative error of at most 0.0038.
Values may be sent and summed in bfloat16 or wider, within the bound.
No kernel may reach another device: no remote copies, remote signals or barrier semaphores. Data moves between devices by JAX's collectives and lax.ppermute only.
A program may use at most 192 MiB of HBM per device.

```python
import math
import jax
import jax.numpy as jnp
from jax import lax

LOADS = 32
LAYERS = 8
NY = 128
MATS = 4
TILE = 2048
NX = 128
PANELS = 32768
SLOTS = 4
N_DEV = 32


def draw_pair_list(key, part):
    num_tiles = PANELS // TILE
    total_pairs = num_tiles * (num_tiles + 1) // 2
    count_key, full_key, order_key = jax.random.split(key, 3)
    lowest = max(1, (SLOTS + 3) // 4)
    counts = jax.random.randint(count_key, (N_DEV,), lowest, SLOTS + 1)
    fullest = jax.random.randint(full_key, (), 0, N_DEV)
    counts = jnp.where(jnp.arange(N_DEV, dtype=jnp.int32) == fullest, SLOTS, counts).astype(jnp.int32)
    offsets = jnp.cumsum(counts) - counts
    ordering = jax.random.permutation(order_key, total_pairs).astype(jnp.int32)
    slot_ids = jnp.arange(SLOTS, dtype=jnp.int32)
    position = jnp.clip(offsets[:, None] + slot_ids[None, :], 0, total_pairs - 1)
    filled = slot_ids[None, :] < counts[:, None]
    chosen = ordering[position]
    tile_ids = jnp.arange(num_tiles, dtype=jnp.int32)
    bases = tile_ids * (tile_ids + 1) // 2
    upper = jnp.sum((bases[None, None, :] <= chosen[:, :, None]).astype(jnp.int32), axis=2) - 1
    lower = chosen - upper * (upper + 1) // 2
    upper = jnp.where(filled, upper, -1)
    lower = jnp.where(filled, lower, -1)
    return jnp.stack([upper.reshape(-1), lower.reshape(-1)], axis=1).astype(jnp.int32)


def touch_ends(values, rng, smallest, top_value):
    extent = values.shape
    place = [jax.random.randint(jax.random.fold_in(rng, axis), (), 0, extent[axis]) for axis in range(len(extent))]
    values = values.at[tuple(place)].set(smallest)
    longest = extent.index(max(extent))
    place[longest] = (place[longest] + 1) % extent[longest]
    return values.at[tuple(place)].set(top_value)


def steps_of(own_key, dims, cuts, low, high):
    gain, own = 1.0, jax.random.fold_in(own_key, 6)
    for axis_at, parts in cuts:
        steps = jnp.exp(jax.random.uniform(jax.random.fold_in(own, axis_at), (parts,), jnp.float32, low / len(cuts), high / len(cuts)))
        gain = gain * jnp.repeat(steps, dims[axis_at] // parts).reshape([-1 if axis == axis_at else 1 for axis in range(len(dims))])
    return gain


def normal_values(rng, extent, deviation, bound, shards=(), kind=jnp.bfloat16):
    array = jax.random.normal(rng, extent, jnp.float32) * deviation
    if len(shards) > 0:
        array = steps_of(rng, extent, shards, -0.22, 0.18) * array
    return jnp.clip(array, min=-bound, max=bound).astype(kind)


def setup_inputs(seed: int = 0) -> dict:
    arg_keys = jax.random.split(jax.random.key(seed), 11)
    field_in = normal_values(arg_keys[0], (LOADS, LAYERS, NX, NY), 1.0, 6.0, ((2, 32),), jnp.float32)
    source = normal_values(arg_keys[1], (LOADS, LAYERS, NX, NY), 2.0, 12.0, ((2, 32),), jnp.float32)
    cell_factor = jnp.clip(jnp.exp(math.log(2.0) - 1.3862944 * jax.random.uniform(arg_keys[2], (LAYERS, NX, NY), jnp.float32) ** steps_of(arg_keys[2], (LAYERS, NX, NY), ((1, 32),), -0.2, 0.2)), 0.5, 2.0)
    layer_material = touch_ends(jax.random.randint(arg_keys[3], (LAYERS,), 0, MATS), jax.random.fold_in(arg_keys[3], 1), 0, MATS - 1).astype(jnp.int32)
    material_scale = jnp.clip(jnp.exp(jax.random.uniform(arg_keys[4], (MATS,), jnp.float32, math.log(0.25), math.log(4.0))), 0.25, 4.0)
    panel_cell = touch_ends(jax.random.randint(arg_keys[5], (PANELS,), 0, NX * NY), jax.random.fold_in(arg_keys[5], 1), 0, (NX * NY) - 1).astype(jnp.int32)
    panel_pos = jnp.clip(jax.random.uniform(arg_keys[6], (3, PANELS), jnp.float32, 0.0, 1.0), 0.0, 1.0)
    panel_area = jnp.clip(jnp.exp(jax.random.uniform(arg_keys[7], (PANELS,), jnp.float32, math.log(0.5), math.log(2.0))), 0.5, 2.0)
    flux_in = normal_values(arg_keys[8], (LOADS, PANELS), 1.0, 6.0, ((1, 32),), jnp.float32)
    pair_list = draw_pair_list(jax.random.fold_in(arg_keys[10], 71), 0)
    return dict(field_in=field_in, source=source, cell_factor=cell_factor, layer_material=layer_material, material_scale=material_scale, panel_cell=panel_cell, panel_pos=panel_pos, panel_area=panel_area, flux_in=flux_in, pair_list=pair_list)


softening = 0.0004
relax_rate = 0.8
update_rate = 0.5
kernel_gain = 0.25

def coefficient(cell_factor, layer_material, material_scale):
    matched = layer_material[:, None] == jnp.arange(material_scale.shape[0], dtype=jnp.int32)[None, :]
    layer_scale = lax.optimization_barrier(jnp.sum(jnp.where(matched, material_scale[None, :], 0.0), axis=1))
    return layer_scale[:, None, None] * cell_factor

def relax_rows(widened, source, conduct):
    centre = widened[:, :, 1:-1, :]
    padded = jnp.pad(centre, ((0, 0), (1, 1), (0, 0), (1, 1)))
    beside = padded[:, 2:, :, 1:-1] + padded[:, :-2, :, 1:-1] + (widened[:, :, 2:, :] + widened[:, :, :-2, :]) + (padded[:, 1:-1, :, 2:] + padded[:, 1:-1, :, :-2])
    applied = conduct * (6.0 * centre - beside) + centre
    return centre + relax_rate * (source - applied) / (6.0 * conduct + 1.0)

def kernel_tile(row_pos, row_area, col_pos, col_area):
    delta_x = row_pos[0][:, None] - col_pos[0][None, :]
    delta_y = row_pos[1][:, None] - col_pos[1][None, :]
    delta_z = row_pos[2][:, None] - col_pos[2][None, :]
    distance = delta_x * delta_x + delta_y * delta_y + delta_z * delta_z
    weight = row_area[:, None] * col_area[None, :]
    return (weight * lax.rsqrt(distance + softening) * (kernel_gain / math.sqrt(TILE))).astype(jnp.bfloat16)

def apply_pairs(pair_rows, flux_half, panel_pos, panel_area, totals):
    load_count = flux_half.shape[0]

    def visit(totals, pair_row):
        upper = pair_row[0]
        lower = pair_row[1]

        def work(totals):
            anchor = jnp.int32(0)
            row_start = (upper * TILE).astype(jnp.int32)
            col_start = (lower * TILE).astype(jnp.int32)
            tile_block = kernel_tile(lax.dynamic_slice(panel_pos, (anchor, row_start), (3, TILE)), lax.dynamic_slice(panel_area, (row_start,), (TILE,)), lax.dynamic_slice(panel_pos, (anchor, col_start), (3, TILE)), lax.dynamic_slice(panel_area, (col_start,), (TILE,)))
            row_flux = lax.dynamic_slice(flux_half, (anchor, row_start), (load_count, TILE))
            col_flux = lax.dynamic_slice(flux_half, (anchor, col_start), (load_count, TILE))
            onward = jnp.dot(row_flux, tile_block, preferred_element_type=jnp.float32)
            current = lax.dynamic_slice(totals, (anchor, col_start), (load_count, TILE))
            totals = lax.dynamic_update_slice(totals, current + onward, (anchor, col_start))

            def transposed(totals):
                backward = lax.dot_general(col_flux, tile_block, (((1,), (1,)), ((), ())), preferred_element_type=jnp.float32)
                present = lax.dynamic_slice(totals, (anchor, row_start), (load_count, TILE))
                return lax.dynamic_update_slice(totals, present + backward, (anchor, row_start))
            return lax.cond(upper != lower, transposed, lambda kept: kept, totals)
        return (lax.cond(upper >= 0, work, lambda kept: kept, totals), None)
    totals, unused = lax.scan(visit, totals, pair_rows)
    return totals

def reference(field_in, source, cell_factor, layer_material, material_scale, panel_cell, panel_pos, panel_area, flux_in, pair_list):
    conduct = coefficient(cell_factor, layer_material, material_scale)
    field_now = field_in
    for repeat in range(2):
        widened = jnp.pad(field_now, ((0, 0), (0, 0), (1, 1), (0, 0)))
        field_now = relax_rows(widened, source, conduct)
    surface_top = field_now[:, -1].astype(jnp.bfloat16)
    flattened = surface_top.reshape(surface_top.shape[0], -1)
    traces = jnp.take(flattened, panel_cell, axis=1)
    flux_half = flux_in.astype(jnp.bfloat16)
    totals = jnp.zeros(flux_in.shape, jnp.float32)
    potential = apply_pairs(pair_list, flux_half, panel_pos, panel_area, totals)
    flux_out = flux_in + update_rate * (traces.astype(jnp.float32) - potential)
    return (field_now, flux_out)
```

```python
import math

import jax
import jax.numpy as jnp
from jax import lax
from jax.experimental import pallas as pl
from jax.experimental.pallas import tpu as pltpu
from jax.sharding import PartitionSpec as P

TILE = 2048

softening = 0.0004
relax_rate = 0.8
update_rate = 0.5
kernel_gain = 0.25

FEATURES = 32
PAIR_ROWS = 16
VMEM_LIMIT = 52 << 20

F32 = jnp.float32
BF16 = jnp.bfloat16


def vmem():
    return pl.BlockSpec(memory_space=pltpu.VMEM)


def smem():
    return pl.BlockSpec(memory_space=pltpu.SMEM)


def call(body, outs, ins, name, scratch=(), cost=None):
    return pl.pallas_call(
        body,
        out_shape=outs,
        in_specs=ins,
        out_specs=[vmem() for _ in outs],
        scratch_shapes=list(scratch),
        name=name,
        cost_estimate=cost,
        compiler_params=pltpu.CompilerParams(vmem_limit_bytes=VMEM_LIMIT),
    )


def halo_kernel(field, source, factor, up, down, *, rows, layers, width):
    lines = field.shape[0] // width

    def line(ref, x, count):
        return ref[pl.ds(x, count, stride=width), :].astype(BF16)

    for out, near, far, edge in (
        (up, width - 2, width - 1, width - 1),
        (down, 0, 1, 0),
    ):
        out[0:lines, :] = line(field, near, lines)
        out[lines : 2 * lines, :] = line(field, far, lines)
        out[2 * lines : 3 * lines, :] = line(source, edge, lines)
        tail = factor[pl.ds(edge, layers, stride=width), :]
        out[3 * lines : rows, :] = jnp.concatenate([tail, tail], axis=0).astype(BF16)


def relax_kernel(material, scale, field, source, factor, above, below, out, top, *, layers, width):
    lines = field.shape[0] // width
    loads = lines // layers
    ny = field.shape[1]
    depth = lax.broadcasted_iota(jnp.int32, (layers, ny), 0)
    lane = lax.broadcasted_iota(jnp.int32, (1, layers, ny), 2)
    level = lax.broadcasted_iota(jnp.int32, (1, layers, ny), 1)
    layer_scale = jnp.zeros((layers, ny), F32)
    for k in range(layers):
        layer_scale = jnp.where(depth == k, scale[material[k]], layer_scale)

    def cube(value):
        return value.reshape(loads, layers, ny)

    def own(ref, x):
        return cube(ref[pl.ds(x, lines, stride=width), :])

    def sent(ref, part):
        return cube(ref[part * lines : (part + 1) * lines, :].astype(F32))

    def sent_factor(ref):
        return ref[3 * lines : 3 * lines + 2 * layers, :].astype(F32)[0:layers]

    fields = {-2: sent(above, 0), -1: sent(above, 1), width: sent(below, 0), width + 1: sent(below, 1)}
    sources = {-1: sent(above, 2), width: sent(below, 2)}
    factors = {-1: sent_factor(above), width: sent_factor(below)}
    for x in range(width):
        fields[x] = own(field, x)
        sources[x] = own(source, x)
        factors[x] = factor[pl.ds(x, layers, stride=width), :]
    conducts = {x: (layer_scale * value)[None] for x, value in factors.items()}
    gains = {x: relax_rate / (6.0 * value + 1.0) for x, value in conducts.items()}

    def sweep(values, x):
        centre = values[x]
        over = jnp.where(level == layers - 1, 0.0, pltpu.roll(centre, layers - 1, 1))
        under = jnp.where(level == 0, 0.0, pltpu.roll(centre, 1, 1))
        right = jnp.where(lane == ny - 1, 0.0, pltpu.roll(centre, ny - 1, 2))
        left = jnp.where(lane == 0, 0.0, pltpu.roll(centre, 1, 2))
        beside = over + under + (values[x + 1] + values[x - 1]) + (right + left)
        applied = conducts[x] * (6.0 * centre - beside) + centre
        return centre + (sources[x] - applied) * gains[x]

    first = {x: sweep(fields, x) for x in range(-1, width + 1)}
    for x in range(width):
        out[pl.ds(x, lines, stride=width), :] = sweep(first, x).reshape(lines, ny)
    for x in range(width):
        rows = pl.ds((layers - 1) * width + x, loads, stride=layers * width)
        top[x * loads : (x + 1) * loads, :] = out[rows, :].astype(BF16)


def pieces(value):
    high = value.astype(BF16).astype(F32)
    rest = value - high
    middle = rest.astype(BF16).astype(F32)
    return high, middle, (rest - middle).astype(BF16).astype(F32)


def row_side(value):
    high, middle, low = pieces(value)
    return [high, high, middle, middle, high, low]


def col_side(value):
    high, middle, low = pieces(value)
    return [high, middle, high, middle, low, high]


def feature_kernel(pos, area, rows_out, cols_out, *, pan, blocks):
    me = lax.axis_index("dev")
    core = lax.rem(me, 2)

    def pick(ref, k, device):
        return ref[k : k + 1, pl.ds(pl.multiple_of(device * pan, pan), pan)]

    def gather(devices):
        lines = [jnp.concatenate([pick(pos, k, d) for d in devices], axis=0) - 0.5 for k in range(3)]
        return lines, jnp.concatenate([pick(area, 0, d) for d in devices], axis=0)

    (x, y, z), weight = gather([2 * g + core for g in range(blocks)])
    scale = 1.0 / (weight * weight)
    terms = [(x * x + y * y + z * z + softening) * scale, scale, x * scale, y * scale, z * scale]
    flat = [piece for term in terms for piece in row_side(term)]
    lanes = rows_out.shape[1]
    for j in range(pan // lanes):
        for f in range(FEATURES):
            start = (j * FEATURES + f) * blocks
            value = flat[f][:, j * lanes : (j + 1) * lanes] if f < len(flat) else jnp.zeros((blocks, lanes), F32)
            rows_out[start : start + blocks, :] = value

    constant = TILE / (kernel_gain * kernel_gain)
    for half, device in enumerate((me, me + 1 - 2 * core)):
        (x, y, z), weight = gather([device])
        scale = constant / (weight * weight)
        terms = [scale, (x * x + y * y + z * z) * scale, -2.0 * x * scale, -2.0 * y * scale, -2.0 * z * scale]
        flat = [piece for term in terms for piece in col_side(term)]
        flat += [jnp.zeros_like(x)] * (FEATURES - len(flat))
        cols_out[:, half * pan : (half + 1) * pan] = jnp.concatenate(flat, axis=0).astype(BF16)


def message_kernel(flux, pairs, partner, out, scratch, *, slots):
    loads, pan = flux.shape
    lanes = out.shape[1]
    for j in range(pan // lanes):
        out[j * loads : (j + 1) * loads, :] = flux[:, j * lanes : (j + 1) * lanes].astype(BF16)
    scratch[...] = jnp.full(scratch.shape, -2.0, F32)
    scratch[0:2, 0:slots] = pairs[...].astype(F32)
    scratch[2:4, 0:slots] = partner[...].astype(F32)
    out[pan // lanes * loads :, :] = scratch[...].astype(BF16)


def add_block(rows, cols, message, start, block, blocks, store, *, loads, pan, wide):
    lanes = message.shape[1]
    parts = [message[pl.ds(start + j * loads, loads), :] for j in range(pan // lanes)]
    flux = jnp.concatenate(parts, axis=1)
    strip = FEATURES * blocks
    parts = [rows[pl.ds(j * strip + block, FEATURES, stride=blocks), :] for j in range(pan // lanes)]
    features = jnp.concatenate(parts, axis=1).astype(BF16)
    for c in range(cols.shape[1] // wide):
        span = slice(c * wide, (c + 1) * wide)
        squared = lax.dot_general(
            features, cols[:, span], (((0,), (0,)), ((), ())), preferred_element_type=F32
        )
        kernel = lax.rsqrt(squared.astype(BF16))
        store(span, jnp.dot(flux, kernel, preferred_element_type=F32))


def near_kernel(rows, cols, *refs, masks, blocks, loads, pan):
    messages, out = refs[:-1], refs[-1]
    me = lax.axis_index("dev")
    for i, (message, mask) in enumerate(zip(messages, masks)):

        def store(span, value, i=i):
            out[i, :, span] = value

        block = lax.shift_right_logical(me ^ mask, 1)
        add_block(rows, cols, message, 0, block, blocks, store, loads=loads, pan=pan, wide=512)


def far_kernel(rows, cols, near, *refs, near_masks, stacks, blocks, loads, pan, size):
    count = len(near_masks)
    firsts, arrived, out = refs[:count], refs[count:-1], refs[-1]
    me = lax.axis_index("dev")
    own = lax.shift_right_logical(me, 1)
    info = size - PAIR_ROWS
    tables = [ref[info:size, :] for ref in firsts]
    for ref, masks in zip(arrived, stacks):
        tables += [ref[i * size + info : (i + 1) * size, :] for i in range(len(masks))]
    first = jnp.concatenate(tables, axis=0).astype(F32)
    total = first.shape[0]
    second = pltpu.roll(first, total - 1, 0)
    index = lax.broadcasted_iota(jnp.int32, first.shape, 0)
    paired = (index % PAIR_ROWS == 0) | (index % PAIR_ROWS == 2)
    mine = own.astype(F32)
    linked = paired & ((first == mine) | (second == mine))
    other = jnp.where(first == mine, second, first).astype(jnp.int32)
    words = []
    for w in range((blocks + 15) // 16):
        inside = linked & (other >= 16 * w) & (other < 16 * (w + 1))
        bit = jnp.left_shift(1, jnp.clip(other - 16 * w, 0, 15)).astype(F32)
        words.append(jnp.sum(jnp.where(inside, bit, 0.0)).astype(jnp.int32))

    def active(block):
        word = words[0]
        for w in range(1, len(words)):
            word = jnp.where(lax.shift_right_logical(block, 4) == w, words[w], word)
        return (lax.shift_right_logical(word, block & 15) & 1) != 0

    gate = [active(lax.shift_right_logical(me ^ mask, 1)).astype(F32) for mask in near_masks]
    out[...] = sum(near[i] * gate[i] for i in range(count))

    def store(span, value):
        out[:, span] += value

    for ref, masks in zip(arrived, stacks):

        @pl.loop(0, len(masks))
        def _(i, ref=ref, masks=masks):
            mask = jnp.int32(masks[0])
            for k in range(1, len(masks)):
                mask = jnp.where(i == k, masks[k], mask)
            block = lax.shift_right_logical(me ^ mask, 1)

            @pl.when(active(block))
            def _():
                start = pl.multiple_of(i * size, 16)
                add_block(rows, cols, ref, start, block, blocks, store, loads=loads, pan=pan, wide=512)


def trace_kernel(potential, cells, partner, *refs, groups, loads, width, pan, ny):
    arrived, outs, table = refs[: len(groups)], refs[len(groups) : -1], refs[-1]
    me = lax.axis_index("dev")
    base = 0
    owners = []
    for ref, masks in zip(arrived, groups):
        count = len(masks) * width * loads
        table[pl.ds(base, count), :] = ref[...].astype(F32)
        base += count
        owners += [me ^ mask for mask in masks]
    lanes = cells.shape[1]
    for half, (cell_ref, out) in enumerate(zip((cells, partner), outs)):
        for pb in range(pan // lanes):
            cell = jnp.broadcast_to(cell_ref[pb : pb + 1, :], (loads, lanes))
            line = lax.div(cell, ny)
            lane = cell - line * ny
            acc = jnp.zeros((loads, lanes), F32)
            for b, owner in enumerate(owners):
                for x in range(width):
                    start = (b * width + x) * loads
                    seen = jnp.take_along_axis(table[start : start + loads, :], lane, axis=1)
                    acc = jnp.where(line == owner * width + x, seen, acc)
            here = half * pan + pb * lanes
            out[:, pb * lanes : (pb + 1) * lanes] = update_rate * (acc - potential[:, here : here + lanes])


def groups_of(size):
    bits = [1 << b for b in range(1, size.bit_length() - 1)]
    low = len(bits) % 2
    split = [bits[i : i + 2] for i in range(low, len(bits), 2)]
    split = ([bits[:low]] if low else []) + split
    phases = []
    for pair in reversed(split):
        phases.append([pair[0]] if len(pair) == 1 else [pair[0], pair[1], pair[0] | pair[1]])
    return phases


def swap(array, mask, size):
    return lax.ppermute(array, "dev", [(i, i ^ mask) for i in range(size)])


def spread(array, phases, size):
    parts = [(array, [0])]
    for masks in phases:
        stack = parts[0][0] if len(parts) == 1 else jnp.concatenate([a for a, _ in parts], axis=0)
        held = [m for _, group in parts for m in group]
        parts = [*parts, *((swap(stack, mask, size), [mask ^ m for m in held]) for mask in masks)]
    return parts


def body(
    field_in,
    source,
    cell_factor,
    layer_material,
    material_scale,
    panel_cell,
    panel_pos,
    panel_area,
    flux_in,
    pair_list,
):
    size = lax.axis_size("dev")
    loads, layers, width, ny = field_in.shape
    pan = flux_in.shape[1]
    slots = pair_list.shape[0]
    blocks = size // 2
    lanes = 128
    lines = loads * layers
    phases = groups_of(size)

    cells = panel_cell.reshape(pan // lanes, lanes)
    pairs = pair_list.T
    partner_cells = swap(cells, 1, size)
    partner_pairs = swap(pairs, 1, size)

    field = field_in.reshape(lines * width, ny)
    load = source.reshape(lines * width, ny)
    factor = cell_factor.reshape(layers * width, ny)
    halo_rows = 3 * lines + 2 * layers
    halo = jax.ShapeDtypeStruct((halo_rows, ny), BF16)
    up, down = call(
        lambda *refs: halo_kernel(*refs, rows=halo_rows, layers=layers, width=width),
        [halo, halo],
        [vmem()] * 3,
        "halo",
    )(field, load, factor)
    above = lax.ppermute(up, "dev", [(i, i + 1) for i in range(size - 1)])
    below = lax.ppermute(down, "dev", [(i + 1, i) for i in range(size - 1)])

    rows, cols = call(
        lambda *refs: feature_kernel(*refs, pan=pan, blocks=blocks),
        [
            jax.ShapeDtypeStruct((pan // lanes * FEATURES * blocks, lanes), F32),
            jax.ShapeDtypeStruct((FEATURES, 2 * pan), BF16),
        ],
        [vmem()] * 2,
        "features",
    )(panel_pos, panel_area.reshape(1, -1))

    message_rows = pan // lanes * loads + PAIR_ROWS
    (message,) = call(
        lambda *refs: message_kernel(*refs, slots=slots),
        [jax.ShapeDtypeStruct((message_rows, lanes), BF16)],
        [vmem()] * 3,
        "message",
        scratch=[pltpu.VMEM((PAIR_ROWS, lanes), F32)],
    )(flux_in, pairs, partner_pairs)
    flux_parts = spread(message, phases, size)
    near_count = 1 + len(phases[0])
    near_parts, far_parts = flux_parts[:near_count], flux_parts[near_count:]

    field_out, top = call(
        lambda *refs: relax_kernel(*refs, layers=layers, width=width),
        [
            jax.ShapeDtypeStruct((lines * width, ny), F32),
            jax.ShapeDtypeStruct((width * loads, ny), BF16),
        ],
        [smem()] * 2 + [vmem()] * 5,
        "relax",
    )(layer_material, material_scale, field, load, factor, above, below)
    top_parts = spread(top, phases, size)

    near_masks = [masks[0] for _, masks in near_parts]
    (near,) = call(
        lambda *refs: near_kernel(*refs, masks=near_masks, blocks=blocks, loads=loads, pan=pan),
        [jax.ShapeDtypeStruct((near_count, loads, 2 * pan), F32)],
        [vmem()] * (2 + near_count),
        "near",
    )(rows, cols, *[a for a, _ in near_parts])
    (potential,) = call(
        lambda *refs: far_kernel(
            *refs,
            near_masks=near_masks,
            stacks=[masks for _, masks in far_parts],
            blocks=blocks,
            loads=loads,
            pan=pan,
            size=message_rows,
        ),
        [jax.ShapeDtypeStruct((loads, 2 * pan), F32)],
        [vmem()] * (3 + near_count + len(far_parts)),
        "far",
    )(rows, cols, near, *[a for a, _ in near_parts], *[a for a, _ in far_parts])

    half = jax.ShapeDtypeStruct((loads, pan), F32)
    kept, given = call(
        lambda *refs: trace_kernel(
            *refs,
            groups=[masks for _, masks in top_parts],
            loads=loads,
            width=width,
            pan=pan,
            ny=ny,
        ),
        [half, half],
        [vmem()] * (3 + len(top_parts)),
        "traces",
        scratch=[pltpu.VMEM((blocks * width * loads, ny), F32)],
    )(potential, cells, partner_cells, *[a for a, _ in top_parts])
    flux_out = flux_in + kept + swap(given, 1, size)
    return (field_out.reshape(field_in.shape), flux_out)


def solution(mesh):
    in_specs = (
        P(None, None, "dev", None),
        P(None, None, "dev", None),
        P(None, "dev", None),
        P(),
        P(),
        P("dev"),
        P(),
        P(),
        P(None, "dev"),
        P("dev", None),
    )
    out_specs = (P(None, None, "dev", None), P(None, "dev"))
    return jax.shard_map(body, mesh=mesh, in_specs=in_specs, out_specs=out_specs, check_vma=False)
```

```python
import jax
import jax.numpy as jnp
from jax import lax
from jax.experimental import pallas as pl
from jax.experimental.pallas import tpu as pltpu
from jax.sharding import PartitionSpec as P


TILE = 2048

softening = 0.0004
relax_rate = 0.8
update_rate = 0.5
kernel_gain = 0.25

FEATURES = 32
PAIR_ROWS = 16
VMEM_LIMIT = 32 << 20

F32 = jnp.float32
BF16 = jnp.bfloat16


def vmem():
    return pl.BlockSpec(memory_space=pltpu.VMEM)


def smem():
    return pl.BlockSpec(memory_space=pltpu.SMEM)


def cost_of(count):
    return pl.CostEstimate(flops=count * 2_500_000_000, bytes_accessed=count << 17, transcendentals=count << 21)


def call(body, outs, ins, scratch=(), cost=None, out_specs=None, aliases=None):
    return pl.pallas_call(
        body,
        out_shape=outs,
        in_specs=ins,
        out_specs=[vmem() for _ in outs] if out_specs is None else out_specs,
        scratch_shapes=list(scratch),
        cost_estimate=cost,
        input_output_aliases=aliases or {},
        compiler_params=pltpu.CompilerParams(vmem_limit_bytes=VMEM_LIMIT),
    )


def prepare_kernel(*refs, rows, layers, width):
    count = 7
    sources, results = refs[:count], refs[count:-2]
    flux, sems = refs[-2:]
    up, down, message, *held = results
    field, source, factor, pairs, pos, area = held
    places = [field, source, factor, flux, pairs, pos, area]
    copies = [pltpu.make_async_copy(a, b, sems.at[i]) for i, (a, b) in enumerate(zip(sources, places))]
    for copy in copies:
        copy.start()
    lanes = message.shape[1]
    loads, pan = flux.shape
    used = pan // lanes * loads
    copies[3].wait()
    for j in range(pan // lanes):
        message[j * loads : (j + 1) * loads, :] = flux[:, j * lanes : (j + 1) * lanes].astype(BF16)
    message[used:, :] = jnp.full((PAIR_ROWS, lanes), -2.0, BF16)
    copies[0].wait()
    copies[1].wait()
    copies[2].wait()
    lines = field.shape[0] // width

    def line(ref, x, count):
        return ref[pl.ds(x, count, stride=width), :].astype(BF16)

    for out, near, far, edge in (
        (up, width - 2, width - 1, width - 1),
        (down, 0, 1, 0),
    ):
        out[0:lines, :] = line(field, near, lines)
        out[lines : 2 * lines, :] = line(field, far, lines)
        out[2 * lines : 3 * lines, :] = line(source, edge, lines)
        tail = factor[pl.ds(edge, layers, stride=width), :]
        out[3 * lines : rows, :] = jnp.concatenate([tail, tail], axis=0).astype(BF16)
    for copy in copies[4:]:
        copy.wait()


def relax_kernel(material, scale, field, source, factor, above, below, out, top, *, layers, width):
    lines = field.shape[0] // width
    loads = lines // layers
    ny = field.shape[1]
    depth = lax.broadcasted_iota(jnp.int32, (layers, ny), 0)
    lane = lax.broadcasted_iota(jnp.int32, (1, layers, ny), 2)
    level = lax.broadcasted_iota(jnp.int32, (1, layers, ny), 1)
    layer_scale = jnp.zeros((layers, ny), F32)
    for k in range(layers):
        layer_scale = jnp.where(depth == k, scale[material[k]], layer_scale)

    def cube(value):
        return value.reshape(loads, layers, ny)

    def own(ref, x):
        return cube(ref[pl.ds(x, lines, stride=width), :])

    def sent(ref, part):
        return cube(ref[part * lines : (part + 1) * lines, :].astype(F32))

    def sent_factor(ref):
        return ref[3 * lines : 3 * lines + 2 * layers, :].astype(F32)[0:layers]

    fields = {-2: sent(above, 0), -1: sent(above, 1), width: sent(below, 0), width + 1: sent(below, 1)}
    sources = {-1: sent(above, 2), width: sent(below, 2)}
    factors = {-1: sent_factor(above), width: sent_factor(below)}
    for x in range(width):
        fields[x] = own(field, x)
        sources[x] = own(source, x)
        factors[x] = factor[pl.ds(x, layers, stride=width), :]
    conducts = {x: (layer_scale * value)[None] for x, value in factors.items()}
    gains = {x: relax_rate / (6.0 * value + 1.0) for x, value in conducts.items()}

    def sweep(values, x):
        centre = values[x]
        over = jnp.where(level == layers - 1, 0.0, pltpu.roll(centre, layers - 1, 1))
        under = jnp.where(level == 0, 0.0, pltpu.roll(centre, 1, 1))
        right = jnp.where(lane == ny - 1, 0.0, pltpu.roll(centre, ny - 1, 2))
        left = jnp.where(lane == 0, 0.0, pltpu.roll(centre, 1, 2))
        beside = over + under + (values[x + 1] + values[x - 1]) + (right + left)
        applied = conducts[x] * (6.0 * centre - beside) + centre
        return centre + (sources[x] - applied) * gains[x]

    first = {x: sweep(fields, x) for x in range(-1, width + 1)}
    for x in range(width):
        out[pl.ds(x, lines, stride=width), :] = sweep(first, x).reshape(lines, ny)
    for x in range(width):
        rows = pl.ds((layers - 1) * width + x, loads, stride=layers * width)
        top[x * loads : (x + 1) * loads, :] = out[rows, :].astype(BF16)


def pieces(value):
    high = value.astype(BF16).astype(F32)
    rest = value - high
    middle = rest.astype(BF16).astype(F32)
    return high, middle, (rest - middle).astype(BF16).astype(F32)


def row_side(value):
    high, middle, low = pieces(value)
    return [high, high, middle, middle, high, low]


def col_side(value):
    high, middle, low = pieces(value)
    return [high, middle, high, middle, low, high]


def feature_kernel(pos, area, rows_out, cols_out, strips, *, pan, blocks):
    me = lax.axis_index("dev")
    core = lax.rem(me, 2)

    def pick(ref, k, device):
        return ref[k : k + 1, pl.ds(pl.multiple_of(device * pan, pan), pan)]

    def gather(devices):
        lines = [jnp.concatenate([pick(pos, k, d) for d in devices], axis=0) - 0.5 for k in range(3)]
        return lines, jnp.concatenate([pick(area, 0, d) for d in devices], axis=0)

    (x, y, z), weight = gather([2 * g + core for g in range(blocks)])
    scale = 1.0 / (weight * weight)
    terms = [(x * x + y * y + z * z + softening) * scale, scale, x * scale, y * scale, z * scale]
    flat = [piece for term in terms for piece in row_side(term)]
    lanes = strips.shape[1]
    strip = FEATURES * blocks
    for j in range(pan // lanes):
        for f in range(FEATURES):
            start = j * strip + f * blocks
            value = flat[f][:, j * lanes : (j + 1) * lanes] if f < len(flat) else jnp.zeros((blocks, lanes), F32)
            strips[start : start + blocks, :] = value
    for g in range(blocks):
        for j in range(pan // lanes):
            value = strips[pl.ds(j * strip + g, FEATURES, stride=blocks), :]
            rows_out[g * FEATURES : (g + 1) * FEATURES, j * lanes : (j + 1) * lanes] = value.astype(BF16)

    constant = TILE / (kernel_gain * kernel_gain)
    for half, device in enumerate((me, me + 1 - 2 * core)):
        (x, y, z), weight = gather([device])
        scale = constant / (weight * weight)
        terms = [scale, (x * x + y * y + z * z) * scale, -2.0 * x * scale, -2.0 * y * scale, -2.0 * z * scale]
        flat = [piece for term in terms for piece in col_side(term)]
        flat += [jnp.zeros_like(x)] * (FEATURES - len(flat))
        cols_out[:, half * pan : (half + 1) * pan] = jnp.concatenate(flat, axis=0).astype(BF16)


def message_kernel(message, pairs, partner, out, scratch):
    slots = pairs.shape[1]
    scratch[...] = jnp.full(scratch.shape, -2.0, F32)
    scratch[0:2, 0:slots] = pairs[...].astype(F32)
    scratch[PAIR_ROWS // 2 : PAIR_ROWS // 2 + 2, 0:slots] = partner[...].astype(F32)
    out[message.shape[0] - PAIR_ROWS :, :] = scratch[...].astype(BF16)


def add_block(rows, cols, message, start, block, store, *, loads, pan, wide):
    lanes = message.shape[1]
    parts = [message[pl.ds(start + j * loads, loads), :] for j in range(pan // lanes)]
    flux = jnp.concatenate(parts, axis=1)
    features = rows[pl.ds(pl.multiple_of(block * FEATURES, FEATURES), FEATURES), :]
    for c in range(cols.shape[1] // wide):
        span = slice(c * wide, (c + 1) * wide)
        squared = lax.dot_general(
            features, cols[:, span], (((0,), (0,)), ((), ())), preferred_element_type=F32
        )
        kernel = lax.rsqrt(squared.astype(BF16))
        store(span, jnp.dot(flux, kernel, preferred_element_type=F32))


def choose(values, i):
    value = jnp.int32(values[0])
    for k in range(1, len(values)):
        value = jnp.where(i == k, values[k], value)
    return value


def near_kernel(rows, cols, stack, out, *, first, masks, loads, pan, size):
    me = lax.axis_index("dev")

    @pl.loop(0, len(masks))
    def _(i):
        block = lax.shift_right_logical(me ^ choose(masks, i), 1)

        def store(span, value):
            out[i, :, span] = value

        start = pl.multiple_of((first + i) * size, 16)
        add_block(rows, cols, stack, start, block, store, loads=loads, pan=pan, wide=512)


def active(words, block):
    word = words[0]
    for w in range(1, words.shape[0]):
        word = jnp.where(lax.shift_right_logical(block, 4) == w, words[w], word)
    return (lax.shift_right_logical(word, block & 15) & 1) != 0


def gate_kernel(*refs, near_masks, near_count, stacks, size):
    nears, tables = refs[:near_count], refs[near_count:-2]
    out, words = refs[-2:]
    me = lax.axis_index("dev")
    own = lax.shift_right_logical(me, 1)
    info = size - PAIR_ROWS
    first = []
    for ref, masks in zip(tables, stacks):
        first += [ref[i * size + info : (i + 1) * size, :] for i in range(len(masks))]
    first = jnp.concatenate(first, axis=0).astype(F32)
    total = first.shape[0]
    second = pltpu.roll(first, total - 1, 0)
    index = lax.broadcasted_iota(jnp.int32, first.shape, 0)
    paired = index % (PAIR_ROWS // 2) == 0
    mine = own.astype(F32)
    linked = paired & ((first == mine) | (second == mine))
    other = jnp.where(first == mine, second, first).astype(jnp.int32)
    for w in range(words.shape[0]):
        inside = linked & (other >= 16 * w) & (other < 16 * (w + 1))
        bit = jnp.left_shift(1, jnp.clip(other - 16 * w, 0, 15)).astype(F32)
        words[w] = jnp.sum(jnp.where(inside, bit, 0.0)).astype(jnp.int32)
    total = None
    i = 0
    for ref in nears:
        for k in range(ref.shape[0]):
            gate = active(words, lax.shift_right_logical(me ^ near_masks[i], 1)).astype(F32)
            value = ref[k] * gate
            total = value if total is None else total + value
            i += 1
    out[...] = total


def far_kernel(words, rows, cols, total, stack, out, *, masks, loads, pan, size):
    me = lax.axis_index("dev")
    out[...] = total[...]

    def store(span, value):
        out[:, span] += value

    @pl.loop(0, len(masks))
    def _(i):
        block = lax.shift_right_logical(me ^ choose(masks, i), 1)

        @pl.when(active(words, block))
        def _():
            start = pl.multiple_of(i * size, 16)
            add_block(rows, cols, stack, start, block, store, loads=loads, pan=pan, wide=512)


def trace_kernel(potential, cells, partner, *refs, groups, loads, width, pan, ny):
    arrived, outs, table = refs[: len(groups)], refs[len(groups) : -1], refs[-1]
    me = lax.axis_index("dev")
    base = 0
    owners = []
    for ref, masks in zip(arrived, groups):
        count = len(masks) * width * loads
        table[pl.ds(base, count), :] = ref[...].astype(F32)
        base += count
        owners += [me ^ mask for mask in masks]
    lanes = cells.shape[1]
    for half, (cell_ref, out) in enumerate(zip((cells, partner), outs)):
        for pb in range(pan // lanes):
            cell = jnp.broadcast_to(cell_ref[pb : pb + 1, :], (loads, lanes))
            line = lax.div(cell, ny)
            lane = cell - line * ny
            acc = jnp.zeros((loads, lanes), F32)
            for b, owner in enumerate(owners):
                for x in range(width):
                    start = (b * width + x) * loads
                    seen = jnp.take_along_axis(table[start : start + loads, :], lane, axis=1)
                    acc = jnp.where(line == owner * width + x, seen, acc)
            here = half * pan + pb * lanes
            out[:, pb * lanes : (pb + 1) * lanes] = update_rate * (acc - potential[:, here : here + lanes])


def groups_of(size):
    bits = [1 << b for b in range(1, size.bit_length() - 1)]
    low = len(bits) % 2
    split = [bits[i : i + 2] for i in range(low, len(bits), 2)]
    split = ([bits[:low]] if low else []) + split
    phases = []
    for pair in reversed(split):
        phases.append([pair[0]] if len(pair) == 1 else [pair[0], pair[1], pair[0] | pair[1]])
    return phases


def swap(array, mask, size):
    return lax.ppermute(array, "dev", [(i, i ^ mask) for i in range(size)])


def spread(array, phases, size):
    parts = [(array, [0])]
    for masks in phases:
        stack = parts[0][0] if len(parts) == 1 else jnp.concatenate([a for a, _ in parts], axis=0)
        held = [m for _, group in parts for m in group]
        sent = [(swap(stack, mask, size), [mask ^ m for m in held]) for mask in masks]
        parts = [*parts, *sent]
    return parts


def program(
    field_in,
    source,
    cell_factor,
    layer_material,
    material_scale,
    panel_cell,
    panel_pos,
    panel_area,
    flux_in,
    pair_list,
):
    size = lax.axis_size("dev")
    loads, layers, width, ny = field_in.shape
    pan = flux_in.shape[1]
    blocks = size // 2
    lanes = 128
    lines = loads * layers
    phases = groups_of(size)

    cells = panel_cell.reshape(pan // lanes, lanes)
    pairs = pair_list.T
    partner_pairs = swap(pairs, 1, size)

    halo_rows = 3 * lines + 2 * layers
    halo = jax.ShapeDtypeStruct((halo_rows, ny), BF16)
    message_rows = pan // lanes * loads + PAIR_ROWS
    wanted = (
        field_in.reshape(lines * width, ny),
        source.reshape(lines * width, ny),
        cell_factor.reshape(layers * width, ny),
        flux_in,
        pairs,
        panel_pos,
        panel_area.reshape(1, -1),
    )
    shapes = [jax.ShapeDtypeStruct(a.shape, a.dtype) for a in wanted]
    up, down, message, field, load, factor, pairs_here, pos, area = call(
        lambda *refs: prepare_kernel(*refs, rows=halo_rows, layers=layers, width=width),
        [halo, halo, jax.ShapeDtypeStruct((message_rows, lanes), BF16), *shapes[:3], *shapes[4:]],
        [pl.BlockSpec(memory_space=pltpu.HBM)] * len(wanted),
        scratch=[pltpu.VMEM(flux_in.shape, F32), pltpu.SemaphoreType.DMA((len(wanted),))],
    )(*[pltpu.with_memory_space_constraint(a, pltpu.HBM) for a in wanted])
    (message,) = call(
        message_kernel,
        [jax.ShapeDtypeStruct((message_rows, lanes), BF16)],
        [vmem()] * 3,
        scratch=[pltpu.VMEM((PAIR_ROWS, lanes), F32)],
        aliases={0: 0},
    )(message, pairs_here, partner_pairs)
    flux_parts = spread(message, phases, size)
    near_count = 1 + len(phases[0])
    near_parts, far_parts = flux_parts[:near_count], flux_parts[near_count:]
    near_stack = jnp.concatenate([a for a, _ in near_parts], axis=0)

    above = lax.ppermute(up, "dev", [(i, i + 1) for i in range(size - 1)])
    below = lax.ppermute(down, "dev", [(i + 1, i) for i in range(size - 1)])
    partner_cells = swap(cells, 1, size)

    rows, cols = call(
        lambda *refs: feature_kernel(*refs, pan=pan, blocks=blocks),
        [
            jax.ShapeDtypeStruct((FEATURES * blocks, pan), BF16),
            jax.ShapeDtypeStruct((FEATURES, 2 * pan), BF16),
        ],
        [vmem()] * 2,
        scratch=[pltpu.VMEM((pan // lanes * FEATURES * blocks, lanes), F32)],
    )(pos, area)

    field_out, top = call(
        lambda *refs: relax_kernel(*refs, layers=layers, width=width),
        [
            jax.ShapeDtypeStruct((lines * width, ny), F32),
            jax.ShapeDtypeStruct((width * loads, ny), BF16),
        ],
        [smem()] * 2 + [vmem()] * 5,
    )(layer_material, material_scale, field, load, factor, above, below)
    top_parts = spread(top, [[bit] for masks in phases for bit in masks[:2]], size)

    wide = jax.ShapeDtypeStruct((loads, 2 * pan), F32)
    near_masks = [masks[0] for _, masks in near_parts]
    nears = []
    first = 0
    for count in (1, 1, near_count - 2):
        masks = near_masks[first : first + count]
        (near,) = call(
            lambda *refs, first=first, masks=masks: near_kernel(
                *refs, first=first, masks=masks, loads=loads, pan=pan, size=message_rows
            ),
            [jax.ShapeDtypeStruct((count, loads, 2 * pan), F32)],
            [vmem()] * 3,
            cost=cost_of(count),
        )(rows, cols, near_stack)
        nears.append(near)
        first += count
    potential, words = call(
        lambda *refs: gate_kernel(
            *refs,
            near_masks=near_masks,
            near_count=len(nears),
            stacks=[masks for _, masks in flux_parts],
            size=message_rows,
        ),
        [wide, jax.ShapeDtypeStruct(((blocks + 15) // 16,), jnp.int32)],
        [vmem()] * (len(nears) + len(flux_parts)),
        out_specs=[vmem(), smem()],
    )(*nears, *[a for a, _ in flux_parts])
    for stack, masks in far_parts:
        (potential,) = call(
            lambda *refs, masks=masks: far_kernel(*refs, masks=masks, loads=loads, pan=pan, size=message_rows),
            [wide],
            [smem()] + [vmem()] * 4,
            cost=cost_of(len(masks)),
            aliases={3: 0},
        )(words, rows, cols, potential, stack)

    half = jax.ShapeDtypeStruct((loads, pan), F32)
    kept, given = call(
        lambda *refs: trace_kernel(
            *refs,
            groups=[masks for _, masks in top_parts],
            loads=loads,
            width=width,
            pan=pan,
            ny=ny,
        ),
        [half, half],
        [vmem()] * (3 + len(top_parts)),
        scratch=[pltpu.VMEM((blocks * width * loads, ny), F32)],
    )(potential, cells, partner_cells, *[a for a, _ in top_parts])
    flux_out = flux_in + kept + swap(given, 1, size)
    return (field_out.reshape(field_in.shape), flux_out)


def solution(mesh):
    in_specs = (
        P(None, None, "dev", None),
        P(None, None, "dev", None),
        P(None, "dev", None),
        P(),
        P(),
        P("dev"),
        P(),
        P(),
        P(None, "dev"),
        P("dev", None),
    )
    out_specs = (P(None, None, "dev", None), P(None, "dev"))
    return jax.shard_map(program, mesh=mesh, in_specs=in_specs, out_specs=out_specs, check_vma=False)
```

```python
import math

import jax
import jax.numpy as jnp
from jax import lax
from jax.experimental import pallas as pl
from jax.experimental.pallas import tpu as pltpu
from jax.sharding import PartitionSpec as P


TILE = 2048

softening = 0.0004
relax_rate = 0.8
update_rate = 0.5
kernel_gain = 0.25

FEATURES = 32
VALUES = 8
PAIR_ROWS = 16
VMEM_LIMIT = 32 << 20

F32 = jnp.float32
BF16 = jnp.bfloat16


def vmem():
    return pl.BlockSpec(memory_space=pltpu.VMEM)


def smem():
    return pl.BlockSpec(memory_space=pltpu.SMEM)


def cost_of(count):
    return pl.CostEstimate(flops=count * 2_500_000_000, bytes_accessed=count << 17, transcendentals=count << 21)


def call(body, outs, ins, scratch=(), cost=None, out_specs=None, aliases=None):
    return pl.pallas_call(
        body,
        out_shape=outs,
        in_specs=ins,
        out_specs=[vmem() for _ in outs] if out_specs is None else out_specs,
        scratch_shapes=list(scratch),
        cost_estimate=cost,
        input_output_aliases=aliases or {},
        compiler_params=pltpu.CompilerParams(vmem_limit_bytes=VMEM_LIMIT),
    )


def prepare_kernel(*refs, rows, layers, width):
    count = 8
    sources, results = refs[:count], refs[count:-5]
    flux, pairs, cells, tile, sems = refs[-5:]
    inner, outer, message, *held = results
    field, source, factor, pos, area = held
    places = [field, source, factor, flux, pairs, cells, pos, area]
    copies = [pltpu.make_async_copy(a, b, sems.at[i]) for i, (a, b) in enumerate(zip(sources, places))]
    for copy in copies:
        copy.start()
    lanes = message.shape[1]
    loads, pan = flux.shape
    slots = pairs.shape[1]
    used = pan // lanes * loads
    for copy in copies[:3]:
        copy.wait()
    lines = field.shape[0] // width
    core = lax.rem(lax.axis_index("dev"), 2)

    def line(ref, x, count):
        return ref[pl.ds(x, count, stride=width), :].astype(BF16)

    for out, upward in ((inner, 1 - core), (outer, core)):
        near = upward * (width - 2)
        edge = upward * (width - 1)
        out[0:lines, :] = line(field, near, lines)
        out[lines : 2 * lines, :] = line(field, near + 1, lines)
        out[2 * lines : 3 * lines, :] = line(source, edge, lines)
        tail = factor[pl.ds(edge, layers, stride=width), :]
        out[3 * lines : rows, :] = jnp.concatenate([tail, tail], axis=0).astype(BF16)
    for copy in copies[3:]:
        copy.wait()
    tile[...] = jnp.full(tile.shape, -2.0, F32)
    tile[0:2, 0:slots] = pairs[...].astype(F32)
    slot_rows = tile[...].astype(BF16)
    inner[rows : rows + PAIR_ROWS, :] = slot_rows
    high = lax.shift_right_logical(cells[...], 8)
    both = jnp.concatenate([high, cells[...] - high * 256], axis=0)
    inner[rows + PAIR_ROWS :, :] = both.astype(F32).astype(BF16)
    weight = area[:, pl.ds(pl.multiple_of(lax.axis_index("dev") * pan, pan), pan)]
    for j in range(pan // lanes):
        span = slice(j * lanes, (j + 1) * lanes)
        half = flux[:, span].astype(BF16).astype(F32)
        message[j * loads : (j + 1) * loads, :] = (half * weight[:, span]).astype(BF16)
    message[used:, :] = slot_rows


def relax_kernel(material, scale, field, source, factor, inner, outer, out, top, *, layers, width):
    lines = field.shape[0] // width
    loads = lines // layers
    ny = field.shape[1]
    depth = lax.broadcasted_iota(jnp.int32, (layers, ny), 0)
    lane = lax.broadcasted_iota(jnp.int32, (1, layers, ny), 2)
    level = lax.broadcasted_iota(jnp.int32, (1, layers, ny), 1)
    layer_scale = jnp.zeros((layers, ny), F32)
    for k in range(layers):
        layer_scale = jnp.where(depth == k, scale[material[k]], layer_scale)

    def cube(value):
        return value.reshape(loads, layers, ny)

    def own(ref, x):
        return cube(ref[pl.ds(x, lines, stride=width), :])

    odd = lax.rem(lax.axis_index("dev"), 2) == 1

    def sent(start, count, above):
        first = inner[start : start + count, :].astype(F32)
        second = outer[start : start + count, :].astype(F32)
        return jnp.where(odd, first, second) if above else jnp.where(odd, second, first)

    def part(i, above):
        return cube(sent(i * lines, lines, above))

    def tail(above):
        return sent(3 * lines, 2 * layers, above)[0:layers]

    fields = {-2: part(0, True), -1: part(1, True), width: part(0, False), width + 1: part(1, False)}
    sources = {-1: part(2, True), width: part(2, False)}
    factors = {-1: tail(True), width: tail(False)}
    for x in range(width):
        fields[x] = own(field, x)
        sources[x] = own(source, x)
        factors[x] = factor[pl.ds(x, layers, stride=width), :]
    conducts = {x: (layer_scale * value)[None] for x, value in factors.items()}
    gains = {x: relax_rate / (6.0 * value + 1.0) for x, value in conducts.items()}

    def sweep(values, x):
        centre = values[x]
        over = jnp.where(level == layers - 1, 0.0, pltpu.roll(centre, layers - 1, 1))
        under = jnp.where(level == 0, 0.0, pltpu.roll(centre, 1, 1))
        right = jnp.where(lane == ny - 1, 0.0, pltpu.roll(centre, ny - 1, 2))
        left = jnp.where(lane == 0, 0.0, pltpu.roll(centre, 1, 2))
        beside = over + under + (values[x + 1] + values[x - 1]) + (right + left)
        applied = conducts[x] * (6.0 * centre - beside) + centre
        return centre + (sources[x] - applied) * gains[x]

    first = {x: sweep(fields, x) for x in range(-1, width + 1)}
    for x in range(width):
        out[pl.ds(x, lines, stride=width), :] = sweep(first, x).reshape(lines, ny)
    for x in range(width):
        rows = pl.ds((layers - 1) * width + x, loads, stride=layers * width)
        top[x * loads : (x + 1) * loads, :] = out[rows, :].astype(BF16)


def pieces(value):
    high = value.astype(BF16).astype(F32)
    rest = value - high
    middle = rest.astype(BF16).astype(F32)
    return high, middle, (rest - middle).astype(BF16).astype(F32)


def row_side(value):
    high, middle, low = pieces(value)
    return [high, high, middle, middle, high, low]


def col_side(value):
    high, middle, low = pieces(value)
    return [high, middle, high, middle, low, high]


def feature_kernel(pos, area, rows_out, row_values, cols_out, col_values, gains, strips, *, pan, blocks):
    me = lax.axis_index("dev")
    core = lax.rem(me, 2)

    def pick(ref, k, device):
        return ref[k : k + 1, pl.ds(pl.multiple_of(device * pan, pan), pan)]

    def gather(devices):
        lines = [jnp.concatenate([pick(pos, k, d) for d in devices], axis=0) - 0.5 for k in range(3)]
        x, y, z = lines
        return lines, x * x + y * y + z * z

    def filled(flat, like, count):
        return flat + [jnp.zeros_like(like)] * (count - len(flat))

    lines, norm = gather([2 * g + core for g in range(blocks)])
    ones = jnp.ones_like(norm)
    norm = norm + softening
    flat = [piece for line in lines for piece in row_side(line)] + [*pieces(norm), ones, ones, ones]
    flat = filled(flat, norm, FEATURES) + filled([*lines, norm], norm, VALUES)
    count = len(flat)
    lanes = strips.shape[1]
    strip = count * blocks
    for j in range(pan // lanes):
        for f in range(count):
            start = j * strip + f * blocks
            strips[start : start + blocks, :] = flat[f][:, j * lanes : (j + 1) * lanes]
    for g in range(blocks):
        for j in range(pan // lanes):
            span = slice(j * lanes, (j + 1) * lanes)
            value = strips[pl.ds(j * strip + g, FEATURES, stride=blocks), :]
            rows_out[g * FEATURES : (g + 1) * FEATURES, span] = value.astype(BF16)
            value = strips[pl.ds(j * strip + FEATURES * blocks + g, VALUES, stride=blocks), :]
            row_values[g * VALUES : (g + 1) * VALUES, span] = value

    for half, device in enumerate((me, me + 1 - 2 * core)):
        span = slice(half * pan, (half + 1) * pan)
        lines, norm = gather([device])
        lines = [-2.0 * line for line in lines]
        ones = jnp.ones_like(norm)
        flat = [piece for line in lines for piece in col_side(line)] + [ones, ones, ones, *pieces(norm)]
        cols_out[:, span] = jnp.concatenate(filled(flat, norm, FEATURES), axis=0).astype(BF16)
        col_values[:, span] = jnp.concatenate(filled([*lines, norm], norm, VALUES), axis=0)
        gains[:, span] = pick(area, 0, device) * (kernel_gain / math.sqrt(TILE))


def message_kernel(message, arrived, out, *, rows):
    half = PAIR_ROWS // 2
    used = message.shape[0] - PAIR_ROWS
    mine = message[used:, :].astype(F32)[0:half]
    other = arrived[rows : rows + PAIR_ROWS, :].astype(F32)[0:half]
    out[used:, :] = jnp.concatenate([mine, other], axis=0).astype(BF16)


def add_block(tables, message, start, block, kernel, store, *, loads, pan, wide=512, step=64):
    rows, row_values, cols, col_values = tables
    lanes = message.shape[1]
    parts = [message[pl.ds(start + j * loads, loads), :] for j in range(pan // lanes)]
    flux = jnp.concatenate(parts, axis=1)
    features = rows[pl.ds(pl.multiple_of(block * FEATURES, FEATURES), FEATURES), :]
    split = pan * 5 // 8
    values = row_values[pl.ds(pl.multiple_of(block * VALUES, VALUES), VALUES), :]
    values = jnp.transpose(values[:, split:])

    def make(span):
        squared = lax.dot_general(
            features[:, :split], cols[:, span], (((0,), (0,)), ((), ())), preferred_element_type=F32
        )
        kernel[:split, span] = lax.rsqrt(squared.astype(BF16))
        col = col_values[:, span]
        for at in range(0, pan - split, step):
            row = values[at : at + step]
            squared = row[:, 0:1] * col[0:1] + row[:, 1:2] * col[1:2] + row[:, 2:3] * col[2:3]
            squared = squared + (row[:, 3:4] + col[3:4])
            kernel[split + at : split + at + step, span] = lax.rsqrt(squared.astype(BF16))

    def apply(span):
        store(span, jnp.dot(flux, kernel[:, span], preferred_element_type=F32))

    spans = [slice(c, c + wide) for c in range(0, cols.shape[1], wide)]
    make(spans[0])
    for before, span in zip(spans, spans[1:]):
        make(span)
        apply(before)
    apply(spans[-1])


def choose(values, i):
    value = jnp.int32(values[0])
    for k in range(1, len(values)):
        value = jnp.where(i == k, values[k], value)
    return value


def near_kernel(*refs, first, masks, loads, pan, size):
    tables, (stack, out, kernel) = refs[:4], refs[4:]
    me = lax.axis_index("dev")

    @pl.loop(0, len(masks))
    def _(i):
        block = lax.shift_right_logical(me ^ choose(masks, i), 1)

        def store(span, value):
            out[i, :, span] = value

        start = pl.multiple_of((first + i) * size, 16)
        add_block(tables, stack, start, block, kernel, store, loads=loads, pan=pan)


def active(words, block):
    word = words[0]
    for w in range(1, words.shape[0]):
        word = jnp.where(lax.shift_right_logical(block, 4) == w, words[w], word)
    return (lax.shift_right_logical(word, block & 15) & 1) != 0


def far_kernel(*refs, near_masks, near_count, stacks, far_count, loads, pan, size):
    tables, nears, stacked = refs[:4], refs[4 : 4 + near_count], refs[4 + near_count : -3]
    out, words, kernel = refs[-3:]
    me = lax.axis_index("dev")
    own = lax.shift_right_logical(me, 1)
    info = size - PAIR_ROWS
    first = []
    for ref, masks in zip(stacked, stacks):
        first += [ref[i * size + info : (i + 1) * size, :] for i in range(len(masks))]
    first = jnp.concatenate(first, axis=0).astype(F32)
    total = first.shape[0]
    second = pltpu.roll(first, total - 1, 0)
    index = lax.broadcasted_iota(jnp.int32, first.shape, 0)
    paired = index % (PAIR_ROWS // 2) == 0
    mine = own.astype(F32)
    linked = paired & ((first == mine) | (second == mine))
    other = jnp.where(first == mine, second, first).astype(jnp.int32)
    for w in range(words.shape[0]):
        inside = linked & (other >= 16 * w) & (other < 16 * (w + 1))
        bit = jnp.left_shift(1, jnp.clip(other - 16 * w, 0, 15)).astype(F32)
        words[w] = jnp.sum(jnp.where(inside, bit, 0.0)).astype(jnp.int32)
    total = None
    i = 0
    for ref in nears:
        for k in range(ref.shape[0]):
            gate = active(words, lax.shift_right_logical(me ^ near_masks[i], 1)).astype(F32)
            value = ref[k] * gate
            total = value if total is None else total + value
            i += 1
    out[...] = total

    def store(span, value):
        out[:, span] += value

    for stack, masks in list(zip(stacked, stacks))[len(stacked) - far_count :]:

        @pl.loop(0, len(masks))
        def _(i, stack=stack, masks=masks):
            block = lax.shift_right_logical(me ^ choose(masks, i), 1)

            @pl.when(active(words, block))
            def _():
                start = pl.multiple_of(i * size, 16)
                add_block(tables, stack, start, block, kernel, store, loads=loads, pan=pan)


def trace_kernel(potential, gains, cells, partner, *refs, groups, loads, width, pan, ny):
    arrived, outs, table = refs[: len(groups)], refs[len(groups) : -1], refs[-1]
    me = lax.axis_index("dev")
    base = 0
    owners = []
    for ref, masks in zip(arrived, groups):
        count = len(masks) * width * loads
        table[pl.ds(base, count), :] = ref[...].astype(F32)
        base += count
        owners += [me ^ mask for mask in masks]
    lanes = cells.shape[1]
    count = pan // lanes
    both = partner[partner.shape[0] - 2 * count :, :].astype(F32)
    theirs = (both[:count] * 256.0 + both[count:]).astype(jnp.int32)
    for half, (mine, out) in enumerate(zip((cells[...], theirs), outs)):
        for pb in range(count):
            cell = jnp.broadcast_to(mine[pb : pb + 1, :], (loads, lanes))
            line = lax.div(cell, ny)
            lane = cell - line * ny
            acc = jnp.zeros((loads, lanes), F32)
            for b, owner in enumerate(owners):
                for x in range(width):
                    start = (b * width + x) * loads
                    seen = jnp.take_along_axis(table[start : start + loads, :], lane, axis=1)
                    acc = jnp.where(line == owner * width + x, seen, acc)
            here = half * pan + pb * lanes
            span = slice(here, here + lanes)
            change = acc - potential[:, span] * gains[:, span]
            out[:, pb * lanes : (pb + 1) * lanes] = update_rate * change


def groups_of(size):
    bits = [1 << b for b in range(1, size.bit_length() - 1)]
    low = len(bits) % 2
    split = [bits[i : i + 2] for i in range(low, len(bits), 2)]
    split = ([bits[:low]] if low else []) + split
    phases = []
    for pair in reversed(split):
        phases.append([pair[0]] if len(pair) == 1 else [pair[0], pair[1], pair[0] | pair[1]])
    return phases


def swap(array, mask, size):
    return lax.ppermute(array, "dev", [(i, i ^ mask) for i in range(size)])


def spread(array, phases, size):
    parts = [(array, [0])]
    for masks in phases:
        stack = parts[0][0] if len(parts) == 1 else jnp.concatenate([a for a, _ in parts], axis=0)
        held = [m for _, group in parts for m in group]
        sent = [(swap(stack, mask, size), [mask ^ m for m in held]) for mask in masks]
        parts = [*parts, *sent]
    return parts


def program(
    field_in,
    source,
    cell_factor,
    layer_material,
    material_scale,
    panel_cell,
    panel_pos,
    panel_area,
    flux_in,
    pair_list,
):
    size = lax.axis_size("dev")
    loads, layers, width, ny = field_in.shape
    pan = flux_in.shape[1]
    blocks = size // 2
    lanes = 128
    lines = loads * layers
    phases = groups_of(size)

    cells = panel_cell.reshape(pan // lanes, lanes)
    halo_rows = 3 * lines + 2 * layers
    inner_rows = halo_rows + PAIR_ROWS + 2 * (pan // lanes)
    message_rows = pan // lanes * loads + PAIR_ROWS
    wanted = (
        field_in.reshape(lines * width, ny),
        source.reshape(lines * width, ny),
        cell_factor.reshape(layers * width, ny),
        flux_in,
        pair_list.T,
        cells,
        panel_pos,
        panel_area.reshape(1, -1),
    )
    shapes = [jax.ShapeDtypeStruct(a.shape, a.dtype) for a in wanted]
    inner, outer, message, field, load, factor, pos, area = call(
        lambda *refs: prepare_kernel(*refs, rows=halo_rows, layers=layers, width=width),
        [
            jax.ShapeDtypeStruct((inner_rows, ny), BF16),
            jax.ShapeDtypeStruct((halo_rows, ny), BF16),
            jax.ShapeDtypeStruct((message_rows, lanes), BF16),
            *shapes[:3],
            *shapes[6:],
        ],
        [pl.BlockSpec(memory_space=pltpu.HBM)] * len(wanted),
        scratch=[
            pltpu.VMEM(flux_in.shape, F32),
            pltpu.VMEM(shapes[4].shape, jnp.int32),
            pltpu.VMEM(cells.shape, jnp.int32),
            pltpu.VMEM((PAIR_ROWS, lanes), F32),
            pltpu.SemaphoreType.DMA((len(wanted),)),
        ],
    )(*[pltpu.with_memory_space_constraint(a, pltpu.HBM) for a in wanted])
    inner = swap(inner, 1, size)
    sides = [(i, i + 1) for i in range(1, size - 1, 2)]
    outer = lax.ppermute(outer, "dev", sides + [(j, i) for i, j in sides])
    (message,) = call(
        lambda *refs: message_kernel(*refs, rows=halo_rows),
        [jax.ShapeDtypeStruct((message_rows, lanes), BF16)],
        [vmem()] * 2,
        aliases={0: 0},
    )(message, inner)
    flux_parts = spread(message, phases, size)
    near_count = 1 + len(phases[0])
    near_parts, far_parts = flux_parts[:near_count], flux_parts[near_count:]
    near_stack = jnp.concatenate([a for a, _ in near_parts], axis=0)

    *tables, gains = call(
        lambda *refs: feature_kernel(*refs, pan=pan, blocks=blocks),
        [
            jax.ShapeDtypeStruct((FEATURES * blocks, pan), BF16),
            jax.ShapeDtypeStruct((VALUES * blocks, pan), F32),
            jax.ShapeDtypeStruct((FEATURES, 2 * pan), BF16),
            jax.ShapeDtypeStruct((VALUES, 2 * pan), F32),
            jax.ShapeDtypeStruct((1, 2 * pan), F32),
        ],
        [vmem()] * 2,
        scratch=[pltpu.VMEM((pan // lanes * (FEATURES + VALUES) * blocks, lanes), F32)],
    )(pos, area)

    field_out, top = call(
        lambda *refs: relax_kernel(*refs, layers=layers, width=width),
        [
            jax.ShapeDtypeStruct((lines * width, ny), F32),
            jax.ShapeDtypeStruct((width * loads, ny), BF16),
        ],
        [smem()] * 2 + [vmem()] * 5,
    )(layer_material, material_scale, field, load, factor, inner, outer)
    top_parts = spread(top, phases, size)

    wide = jax.ShapeDtypeStruct((loads, 2 * pan), F32)
    strip = pltpu.VMEM((pan, 2 * pan), BF16)
    near_masks = [masks[0] for _, masks in near_parts]
    nears = []
    for first, masks, stack in ((0, near_masks[:1], message), (1, near_masks[1:], near_stack)):
        (near,) = call(
            lambda *refs, first=first, masks=masks: near_kernel(
                *refs, first=first, masks=masks, loads=loads, pan=pan, size=message_rows
            ),
            [jax.ShapeDtypeStruct((len(masks), loads, 2 * pan), F32)],
            [vmem()] * 5,
            scratch=[strip],
            cost=cost_of(len(masks)),
        )(*tables, stack)
        nears.append(near)
    (potential,) = call(
        lambda *refs: far_kernel(
            *refs,
            near_masks=near_masks,
            near_count=len(nears),
            stacks=[masks for _, masks in flux_parts],
            far_count=len(far_parts),
            loads=loads,
            pan=pan,
            size=message_rows,
        ),
        [wide],
        [vmem()] * (4 + len(nears) + len(flux_parts)),
        scratch=[pltpu.SMEM(((blocks + 15) // 16,), jnp.int32), strip],
        cost=cost_of(blocks - near_count),
    )(*tables, *nears, *[a for a, _ in flux_parts])

    half = jax.ShapeDtypeStruct((loads, pan), F32)
    kept, given = call(
        lambda *refs: trace_kernel(
            *refs,
            groups=[masks for _, masks in top_parts],
            loads=loads,
            width=width,
            pan=pan,
            ny=ny,
        ),
        [half, half],
        [vmem()] * (4 + len(top_parts)),
        scratch=[pltpu.VMEM((blocks * width * loads, ny), F32)],
    )(potential, gains, cells, inner, *[a for a, _ in top_parts])
    flux_out = flux_in + kept + swap(given, 1, size)
    return (field_out.reshape(field_in.shape), flux_out)


def solution(mesh):
    in_specs = (
        P(None, None, "dev", None),
        P(None, None, "dev", None),
        P(None, "dev", None),
        P(),
        P(),
        P("dev"),
        P(),
        P(),
        P(None, "dev"),
        P("dev", None),
    )
    out_specs = (P(None, None, "dev", None), P(None, "dev"))
    return jax.shard_map(program, mesh=mesh, in_specs=in_specs, out_specs=out_specs, check_vma=False)
```

```python
import math

import jax
import jax.numpy as jnp
from jax import lax
from jax.experimental import pallas as pl
from jax.experimental.pallas import tpu as pltpu
from jax.sharding import PartitionSpec as P


TILE = 2048

softening = 0.0004
relax_rate = 0.8
update_rate = 0.5
kernel_gain = 0.25

FEATURES = 32
VALUES = 8
PAIR_ROWS = 16
VMEM_LIMIT = 32 << 20

F32 = jnp.float32
BF16 = jnp.bfloat16


def vmem():
    return pl.BlockSpec(memory_space=pltpu.VMEM)


def cost_of(count):
    return pl.CostEstimate(flops=count * 2_500_000_000, bytes_accessed=count << 17, transcendentals=count << 21)


def call(body, outs, ins, scratch=(), cost=None, out_specs=None, aliases=None):
    return pl.pallas_call(
        body,
        out_shape=outs,
        in_specs=ins,
        out_specs=[vmem() for _ in outs] if out_specs is None else out_specs,
        scratch_shapes=list(scratch),
        cost_estimate=cost,
        input_output_aliases=aliases or {},
        compiler_params=pltpu.CompilerParams(vmem_limit_bytes=VMEM_LIMIT),
    )


def prepare_kernel(*refs, rows, layers, width):
    count = 10
    sources, results = refs[:count], refs[count:-8]
    raw, material, scale, flux, pairs, cells, tile, sems = refs[-8:]
    inner, outer, message, *held = results
    field, source, factor, pos, area = held
    places = [field, source, raw, material, scale, flux, pairs, cells, pos, area]
    copies = [pltpu.make_async_copy(a, b, sems.at[i]) for i, (a, b) in enumerate(zip(sources, places))]
    for copy in copies:
        copy.start()
    lanes = message.shape[1]
    loads, pan = flux.shape
    slots = pairs.shape[1]
    used = pan // lanes * loads
    for copy in copies[:5]:
        copy.wait()
    lines = field.shape[0] // width
    depth = lax.broadcasted_iota(jnp.int32, (layers, lanes), 0)
    layer_scale = jnp.zeros((layers, lanes), F32)
    for k in range(layers):
        layer_scale = jnp.where(depth == k, scale[material[k]], layer_scale)
    for x in range(width):
        own = pl.ds(x, layers, stride=width)
        factor[own, :] = layer_scale * raw[own, :]
    core = lax.rem(lax.axis_index("dev"), 2)

    def line(ref, x, count):
        return ref[pl.ds(x, count, stride=width), :].astype(BF16)

    for out, upward in ((inner, 1 - core), (outer, core)):
        near = upward * (width - 2)
        edge = upward * (width - 1)
        out[0:lines, :] = line(field, near, lines)
        out[lines : 2 * lines, :] = line(field, near + 1, lines)
        out[2 * lines : 3 * lines, :] = line(source, edge, lines)
        tail = factor[pl.ds(edge, layers, stride=width), :]
        out[3 * lines : rows, :] = jnp.concatenate([tail, tail], axis=0).astype(BF16)
    for copy in copies[5:]:
        copy.wait()
    tile[...] = jnp.full(tile.shape, -2.0, F32)
    tile[0:2, 0:slots] = pairs[...].astype(F32)
    slot_rows = tile[...].astype(BF16)
    inner[rows : rows + PAIR_ROWS, :] = slot_rows
    high = lax.shift_right_logical(cells[...], 8)
    both = jnp.concatenate([high, cells[...] - high * 256], axis=0)
    inner[rows + PAIR_ROWS :, :] = both.astype(F32).astype(BF16)
    weight = area[:, pl.ds(pl.multiple_of(lax.axis_index("dev") * pan, pan), pan)]
    for j in range(pan // lanes):
        span = slice(j * lanes, (j + 1) * lanes)
        half = flux[:, span].astype(BF16).astype(F32)
        message[j * loads : (j + 1) * loads, :] = (half * weight[:, span]).astype(BF16)
    message[used:, :] = slot_rows


def relax_kernel(field, source, conduct, inner, outer, out, top, *, layers, width):
    lines = field.shape[0] // width
    loads = lines // layers
    ny = field.shape[1]
    lane = lax.broadcasted_iota(jnp.int32, (1, layers, ny), 2)
    level = lax.broadcasted_iota(jnp.int32, (1, layers, ny), 1)

    def cube(value):
        return value.reshape(loads, layers, ny)

    def own(ref, x):
        return cube(ref[pl.ds(x, lines, stride=width), :])

    odd = lax.rem(lax.axis_index("dev"), 2) == 1

    def sent(start, count, above):
        first = inner[start : start + count, :].astype(F32)
        second = outer[start : start + count, :].astype(F32)
        return jnp.where(odd, first, second) if above else jnp.where(odd, second, first)

    def part(i, above):
        return cube(sent(i * lines, lines, above))

    def tail(above):
        return sent(3 * lines, 2 * layers, above)[0:layers]

    fields = {-2: part(0, True), -1: part(1, True), width: part(0, False), width + 1: part(1, False)}
    sources = {-1: part(2, True), width: part(2, False)}
    conducts = {-1: tail(True)[None], width: tail(False)[None]}
    for x in range(width):
        fields[x] = own(field, x)
        sources[x] = own(source, x)
        conducts[x] = conduct[pl.ds(x, layers, stride=width), :][None]
    gains = {x: relax_rate / (6.0 * value + 1.0) for x, value in conducts.items()}

    def sweep(values, x):
        centre = values[x]
        over = jnp.where(level == layers - 1, 0.0, pltpu.roll(centre, layers - 1, 1))
        under = jnp.where(level == 0, 0.0, pltpu.roll(centre, 1, 1))
        right = jnp.where(lane == ny - 1, 0.0, pltpu.roll(centre, ny - 1, 2))
        left = jnp.where(lane == 0, 0.0, pltpu.roll(centre, 1, 2))
        beside = over + under + (values[x + 1] + values[x - 1]) + (right + left)
        applied = conducts[x] * (6.0 * centre - beside) + centre
        return centre + (sources[x] - applied) * gains[x]

    first = {x: sweep(fields, x) for x in range(-1, width + 1)}
    for x in range(width):
        out[pl.ds(x, lines, stride=width), :] = sweep(first, x).reshape(lines, ny)
    for x in range(width):
        rows = pl.ds((layers - 1) * width + x, loads, stride=layers * width)
        top[x * loads : (x + 1) * loads, :] = out[rows, :].astype(BF16)


def pieces(value):
    high = value.astype(BF16).astype(F32)
    rest = value - high
    middle = rest.astype(BF16).astype(F32)
    return high, middle, (rest - middle).astype(BF16).astype(F32)


def row_side(value):
    high, middle, low = pieces(value)
    return [high, high, middle, middle, high, low]


def col_side(value):
    high, middle, low = pieces(value)
    return [high, middle, high, middle, low, high]


def feature_kernel(pos, area, rows_out, row_values, cols_out, col_values, gains, strips, *, pan, blocks):
    me = lax.axis_index("dev")
    core = lax.rem(me, 2)

    def pick(ref, k, device):
        return ref[k : k + 1, pl.ds(pl.multiple_of(device * pan, pan), pan)]

    def gather(devices):
        lines = [jnp.concatenate([pick(pos, k, d) for d in devices], axis=0) - 0.5 for k in range(3)]
        x, y, z = lines
        return lines, x * x + y * y + z * z

    def filled(flat, like, count):
        return flat + [jnp.zeros_like(like)] * (count - len(flat))

    lines, norm = gather([2 * g + core for g in range(blocks)])
    ones = jnp.ones_like(norm)
    norm = norm + softening
    flat = [piece for line in lines for piece in row_side(line)] + [*pieces(norm), ones, ones, ones]
    flat = filled(flat, norm, FEATURES) + filled([*lines, norm], norm, VALUES)
    count = len(flat)
    lanes = strips.shape[1]
    strip = count * blocks
    for j in range(pan // lanes):
        for f in range(count):
            start = j * strip + f * blocks
            strips[start : start + blocks, :] = flat[f][:, j * lanes : (j + 1) * lanes]
    for g in range(blocks):
        for j in range(pan // lanes):
            span = slice(j * lanes, (j + 1) * lanes)
            value = strips[pl.ds(j * strip + g, FEATURES, stride=blocks), :]
            rows_out[g * FEATURES : (g + 1) * FEATURES, span] = value.astype(BF16)
            value = strips[pl.ds(j * strip + FEATURES * blocks + g, VALUES, stride=blocks), :]
            row_values[g * VALUES : (g + 1) * VALUES, span] = value

    for half, device in enumerate((me, me + 1 - 2 * core)):
        span = slice(half * pan, (half + 1) * pan)
        lines, norm = gather([device])
        lines = [-2.0 * line for line in lines]
        ones = jnp.ones_like(norm)
        flat = [piece for line in lines for piece in col_side(line)] + [ones, ones, ones, *pieces(norm)]
        cols_out[:, span] = jnp.concatenate(filled(flat, norm, FEATURES), axis=0).astype(BF16)
        col_values[:, span] = jnp.concatenate(filled([*lines, norm], norm, VALUES), axis=0)
        gains[:, span] = pick(area, 0, device) * (kernel_gain / math.sqrt(TILE))


def message_kernel(message, arrived, out, *, rows):
    half = PAIR_ROWS // 2
    used = message.shape[0] - PAIR_ROWS
    mine = message[used:, :].astype(F32)[0:half]
    other = arrived[rows : rows + PAIR_ROWS, :].astype(F32)[0:half]
    out[used:, :] = jnp.concatenate([mine, other], axis=0).astype(BF16)


def add_block(tables, message, start, block, kernel, store, *, loads, pan, wide=512, step=64):
    rows, row_values, cols, col_values = tables
    lanes = message.shape[1]
    parts = [message[pl.ds(start + j * loads, loads), :] for j in range(pan // lanes)]
    flux = jnp.concatenate(parts, axis=1)
    features = rows[pl.ds(pl.multiple_of(block * FEATURES, FEATURES), FEATURES), :]
    split = pan * 5 // 8
    values = row_values[pl.ds(pl.multiple_of(block * VALUES, VALUES), VALUES), :]
    values = jnp.transpose(values[:, split:])

    def make(span):
        squared = lax.dot_general(
            features[:, :split], cols[:, span], (((0,), (0,)), ((), ())), preferred_element_type=F32
        )
        kernel[:split, span] = lax.rsqrt(squared.astype(BF16))
        col = col_values[:, span]
        for at in range(0, pan - split, step):
            row = values[at : at + step]
            squared = row[:, 0:1] * col[0:1] + row[:, 1:2] * col[1:2] + row[:, 2:3] * col[2:3]
            squared = squared + (row[:, 3:4] + col[3:4])
            kernel[split + at : split + at + step, span] = lax.rsqrt(squared.astype(BF16))

    def apply(span):
        store(span, jnp.dot(flux, kernel[:, span], preferred_element_type=F32))

    spans = [slice(c, c + wide) for c in range(0, cols.shape[1], wide)]
    make(spans[0])
    for before, span in zip(spans, spans[1:]):
        make(span)
        apply(before)
    apply(spans[-1])


def choose(values, i):
    value = jnp.int32(values[0])
    for k in range(1, len(values)):
        value = jnp.where(i == k, values[k], value)
    return value


def near_kernel(*refs, masks, loads, pan, size):
    tables, (stack, out, kernel) = refs[:4], refs[4:]
    me = lax.axis_index("dev")

    @pl.loop(0, len(masks))
    def _(i):
        block = lax.shift_right_logical(me ^ choose(masks, i), 1)

        def store(span, value):
            out[i, :, span] = value

        start = pl.multiple_of(i * size, 16)
        add_block(tables, stack, start, block, kernel, store, loads=loads, pan=pan)


def active(words, block):
    word = words[0]
    for w in range(1, words.shape[0]):
        word = jnp.where(lax.shift_right_logical(block, 4) == w, words[w], word)
    return (lax.shift_right_logical(word, block & 15) & 1) != 0


def far_kernel(*refs, near_masks, near_count, stacks, far_count, loads, pan, size):
    tables, nears, stacked = refs[:4], refs[4 : 4 + near_count], refs[4 + near_count : -3]
    out, words, kernel = refs[-3:]
    me = lax.axis_index("dev")
    own = lax.shift_right_logical(me, 1)
    info = size - PAIR_ROWS
    first = []
    for ref, masks in zip(stacked, stacks):
        first += [ref[i * size + info : (i + 1) * size, :] for i in range(len(masks))]
    first = jnp.concatenate(first, axis=0).astype(F32)
    total = first.shape[0]
    second = pltpu.roll(first, total - 1, 0)
    index = lax.broadcasted_iota(jnp.int32, first.shape, 0)
    paired = index % (PAIR_ROWS // 2) == 0
    mine = own.astype(F32)
    linked = paired & ((first == mine) | (second == mine))
    other = jnp.where(first == mine, second, first).astype(jnp.int32)
    for w in range(words.shape[0]):
        inside = linked & (other >= 16 * w) & (other < 16 * (w + 1))
        bit = jnp.left_shift(1, jnp.clip(other - 16 * w, 0, 15)).astype(F32)
        words[w] = jnp.sum(jnp.where(inside, bit, 0.0)).astype(jnp.int32)
    total = None
    i = 0
    for ref in nears:
        for k in range(ref.shape[0]):
            gate = active(words, lax.shift_right_logical(me ^ near_masks[i], 1)).astype(F32)
            value = ref[k] * gate
            total = value if total is None else total + value
            i += 1
    out[...] = total

    def store(span, value):
        out[:, span] += value

    for stack, masks in list(zip(stacked, stacks))[len(stacked) - far_count :]:

        @pl.loop(0, len(masks))
        def _(i, stack=stack, masks=masks):
            block = lax.shift_right_logical(me ^ choose(masks, i), 1)

            @pl.when(active(words, block))
            def _():
                start = pl.multiple_of(i * size, 16)
                add_block(tables, stack, start, block, kernel, store, loads=loads, pan=pan)


def trace_kernel(potential, gains, cells, partner, *refs, groups, loads, width, pan, ny):
    arrived, outs, table = refs[: len(groups)], refs[len(groups) : -1], refs[-1]
    me = lax.axis_index("dev")
    base = 0
    owners = []
    for ref, masks in zip(arrived, groups):
        count = len(masks) * width * loads
        table[pl.ds(base, count), :] = ref[...].astype(F32)
        base += count
        owners += [me ^ mask for mask in masks]
    lanes = cells.shape[1]
    count = pan // lanes
    both = partner[partner.shape[0] - 2 * count :, :].astype(F32)
    theirs = (both[:count] * 256.0 + both[count:]).astype(jnp.int32)
    for half, (mine, out) in enumerate(zip((cells[...], theirs), outs)):
        for pb in range(count):
            cell = jnp.broadcast_to(mine[pb : pb + 1, :], (loads, lanes))
            line = lax.div(cell, ny)
            lane = cell - line * ny
            acc = jnp.zeros((loads, lanes), F32)
            for b, owner in enumerate(owners):
                for x in range(width):
                    start = (b * width + x) * loads
                    seen = jnp.take_along_axis(table[start : start + loads, :], lane, axis=1)
                    acc = jnp.where(line == owner * width + x, seen, acc)
            here = half * pan + pb * lanes
            span = slice(here, here + lanes)
            change = acc - potential[:, span] * gains[:, span]
            out[:, pb * lanes : (pb + 1) * lanes] = update_rate * change


def groups_of(size):
    bits = [1 << b for b in range(1, size.bit_length() - 1)]
    low = len(bits) % 2
    split = [bits[i : i + 2] for i in range(low, len(bits), 2)]
    split = ([bits[:low]] if low else []) + split
    phases = []
    for pair in reversed(split):
        phases.append([pair[0]] if len(pair) == 1 else [pair[0], pair[1], pair[0] | pair[1]])
    return phases


def phases_of(size):
    first, *others = groups_of(size)
    return [[mask] for mask in first[:2]] + others


def swap(array, mask, size):
    return lax.ppermute(array, "dev", [(i, i ^ mask) for i in range(size)])


def spread(array, phases, size):
    parts = [(array, [0])]
    for masks in phases:
        stack = parts[0][0] if len(parts) == 1 else jnp.concatenate([a for a, _ in parts], axis=0)
        held = [m for _, group in parts for m in group]
        sent = [(swap(stack, mask, size), [mask ^ m for m in held]) for mask in masks]
        parts = [*parts, *sent]
    return parts


def program(
    field_in,
    source,
    cell_factor,
    layer_material,
    material_scale,
    panel_cell,
    panel_pos,
    panel_area,
    flux_in,
    pair_list,
):
    size = lax.axis_size("dev")
    loads, layers, width, ny = field_in.shape
    pan = flux_in.shape[1]
    blocks = size // 2
    lanes = 128
    lines = loads * layers
    phases = phases_of(size)

    cells = panel_cell.reshape(pan // lanes, lanes)
    halo_rows = 3 * lines + 2 * layers
    inner_rows = halo_rows + PAIR_ROWS + 2 * (pan // lanes)
    message_rows = pan // lanes * loads + PAIR_ROWS
    wanted = (
        field_in.reshape(lines * width, ny),
        source.reshape(lines * width, ny),
        cell_factor.reshape(layers * width, ny),
        layer_material,
        material_scale,
        flux_in,
        pair_list.T,
        cells,
        panel_pos,
        panel_area.reshape(1, -1),
    )
    shapes = [jax.ShapeDtypeStruct(a.shape, a.dtype) for a in wanted]
    inner, outer, message, field, load, conduct, pos, area = call(
        lambda *refs: prepare_kernel(*refs, rows=halo_rows, layers=layers, width=width),
        [
            jax.ShapeDtypeStruct((inner_rows, ny), BF16),
            jax.ShapeDtypeStruct((halo_rows, ny), BF16),
            jax.ShapeDtypeStruct((message_rows, lanes), BF16),
            *shapes[:3],
            *shapes[8:],
        ],
        [pl.BlockSpec(memory_space=pltpu.HBM)] * len(wanted),
        scratch=[
            pltpu.VMEM(shapes[2].shape, F32),
            pltpu.SMEM(layer_material.shape, jnp.int32),
            pltpu.SMEM(material_scale.shape, F32),
            pltpu.VMEM(flux_in.shape, F32),
            pltpu.VMEM(pair_list.shape[::-1], jnp.int32),
            pltpu.VMEM(cells.shape, jnp.int32),
            pltpu.VMEM((PAIR_ROWS, lanes), F32),
            pltpu.SemaphoreType.DMA((len(wanted),)),
        ],
    )(*[pltpu.with_memory_space_constraint(a, pltpu.HBM) for a in wanted])
    inner = swap(inner, 1, size)
    sides = [(i, i + 1) for i in range(1, size - 1, 2)]
    outer = lax.ppermute(outer, "dev", sides + [(j, i) for i, j in sides])
    (message,) = call(
        lambda *refs: message_kernel(*refs, rows=halo_rows),
        [jax.ShapeDtypeStruct((message_rows, lanes), BF16)],
        [vmem()] * 2,
        aliases={0: 0},
    )(message, inner)
    flux_parts = spread(message, phases, size)
    near_count = 3
    near_parts, far_parts = flux_parts[:near_count], flux_parts[near_count:]

    *tables, gains = call(
        lambda *refs: feature_kernel(*refs, pan=pan, blocks=blocks),
        [
            jax.ShapeDtypeStruct((FEATURES * blocks, pan), BF16),
            jax.ShapeDtypeStruct((VALUES * blocks, pan), F32),
            jax.ShapeDtypeStruct((FEATURES, 2 * pan), BF16),
            jax.ShapeDtypeStruct((VALUES, 2 * pan), F32),
            jax.ShapeDtypeStruct((1, 2 * pan), F32),
        ],
        [vmem()] * 2,
        scratch=[pltpu.VMEM((pan // lanes * (FEATURES + VALUES) * blocks, lanes), F32)],
    )(pos, area)

    field_out, top = call(
        lambda *refs: relax_kernel(*refs, layers=layers, width=width),
        [
            jax.ShapeDtypeStruct((lines * width, ny), F32),
            jax.ShapeDtypeStruct((width * loads, ny), BF16),
        ],
        [vmem()] * 5,
    )(field, load, conduct, inner, outer)
    top_parts = spread(top, phases, size)

    wide = jax.ShapeDtypeStruct((loads, 2 * pan), F32)
    strip = pltpu.VMEM((pan, 2 * pan), BF16)
    near_masks = [mask for _, masks in near_parts for mask in masks]
    nears = []
    for masks, stack in (
        (near_masks[:1], message),
        (near_masks[1:2], near_parts[1][0]),
        (near_masks[2:], near_parts[2][0]),
    ):
        (near,) = call(
            lambda *refs, masks=masks: near_kernel(
                *refs, masks=masks, loads=loads, pan=pan, size=message_rows
            ),
            [jax.ShapeDtypeStruct((len(masks), loads, 2 * pan), F32)],
            [vmem()] * 5,
            scratch=[strip],
            cost=cost_of(len(masks)),
        )(*tables, stack)
        nears.append(near)
    (potential,) = call(
        lambda *refs: far_kernel(
            *refs,
            near_masks=near_masks,
            near_count=len(nears),
            stacks=[masks for _, masks in flux_parts],
            far_count=len(far_parts),
            loads=loads,
            pan=pan,
            size=message_rows,
        ),
        [wide],
        [vmem()] * (4 + len(nears) + len(flux_parts)),
        scratch=[pltpu.SMEM(((blocks + 15) // 16,), jnp.int32), strip],
        cost=cost_of(blocks - len(near_masks)),
    )(*tables, *nears, *[a for a, _ in flux_parts])

    half = jax.ShapeDtypeStruct((loads, pan), F32)
    kept, given = call(
        lambda *refs: trace_kernel(
            *refs,
            groups=[masks for _, masks in top_parts],
            loads=loads,
            width=width,
            pan=pan,
            ny=ny,
        ),
        [half, half],
        [vmem()] * (4 + len(top_parts)),
        scratch=[pltpu.VMEM((blocks * width * loads, ny), F32)],
    )(potential, gains, cells, inner, *[a for a, _ in top_parts])
    flux_out = flux_in + kept + swap(given, 1, size)
    return (field_out.reshape(field_in.shape), flux_out)


def solution(mesh):
    in_specs = (
        P(None, None, "dev", None),
        P(None, None, "dev", None),
        P(None, "dev", None),
        P(),
        P(),
        P("dev"),
        P(),
        P(),
        P(None, "dev"),
        P("dev", None),
    )
    out_specs = (P(None, None, "dev", None), P(None, "dev"))
    return jax.shard_map(program, mesh=mesh, in_specs=in_specs, out_specs=out_specs, check_vma=False)
```
